32 devices in a mesh: dp: 32 (over z, y, x, core).
Axes of the slice: x: 2, y: 2, z: 4, core: 2. Of those that a mesh axis runs over, the one named last changes fastest.
Arguments:
- hidden_in: bfloat16 [4096, 960], P('dp')
- seg_start: int32 [4096], P('dp'), may hold values from 0 to 128, as said below
- w_query: bfloat16 [921600], P('dp'), may hold values from -0.1875 to 0.1875
- w_key: bfloat16 [307200], P('dp'), may hold values from -0.1875 to 0.1875
- w_value: bfloat16 [307200], P('dp'), may hold values from -0.1875 to 0.1875
- w_output: bfloat16 [921600], P('dp'), may hold values from -0.5 to 0.5
- w_gate: bfloat16 [2457600], P('dp'), may hold values from -0.1875 to 0.1875
- w_up: bfloat16 [2457600], P('dp'), may hold values from -0.1875 to 0.1875
- w_down: bfloat16 [2457600], P('dp'), may hold values from -0.25 to 0.25
- norm_gains: bfloat16 [1920], P('dp'), may hold values from 0.5 to 1.5
- cotangent: bfloat16 [4096, 960], P('dp'), may hold values from -6 to 6
Outputs:
- hidden_out: bfloat16 [4096, 960], P('dp')
- grad_in: float32 [4096, 960], P('dp')
- grad_query: float32 [921600], P('dp')
- grad_key: float32 [307200], P('dp')
- grad_value: float32 [307200], P('dp')
- grad_output: float32 [921600], P('dp')
- grad_gate: float32 [2457600], P('dp')
- grad_up: float32 [2457600], P('dp')
- grad_down: float32 [2457600], P('dp')
- grad_gains: float32 [1920], P('dp')
The draws below stay inside these ranges and needn't reach their ends.
Inputs may be any that keep to these rules, and one draw needn't show every extreme that they name: `seg_start`: within each device's block of 128 slots the live slots come first and every later slot holds 128; a live slot's value is the index in the block of the first slot of its sequence, equal for all slots of that sequence and at most the slot's own index. Some device's block has no empty slot.
All inputs are finite; a program needn't handle non-finite values.
Results may differ from the reference program's by a relative error of at most 0.012.
Values may be sent and summed in bfloat16 or wider, within the bound.
No kernel may reach another device: no remote copies, remote signals or barrier semaphores. Data moves between devices by JAX's collectives and lax.ppermute only.
A program may use at most 256 MiB of HBM per device.

```python
import math
import jax
import jax.numpy as jnp
from jax import lax

D = 960
HEADS = 15
KVH = 5
HDIM = 64
FF = 2560
CAP = 128
TOKENS = 4096
GAINS = 1920
N_DP = 32


def draw_hidden_in(key, part):
    key_base, key_rows, key_cols = jax.random.split(key, 3)
    base_vals = jnp.clip(jax.random.normal(key_base, (TOKENS, D), jnp.float32), -5.0, 5.0)
    row_scale = jnp.exp(jax.random.uniform(key_rows, (TOKENS, 1), jnp.float32, -1.15, 1.15))
    col_scale = jnp.exp(jax.random.uniform(key_cols, (1, D), jnp.float32, -1.15, 1.15))
    return (base_vals * row_scale * col_scale).astype(jnp.bfloat16)


def draw_seg_start(key, part):
    buffers = TOKENS // CAP
    key_live, key_full, key_marks = jax.random.split(key, 3)
    spread = jax.random.randint(key_live, (buffers,), 0, CAP, dtype=jnp.int32)
    live_count = jnp.maximum(CAP // 8, spread * spread // CAP)
    full_one = jax.random.randint(key_full, (), 0, buffers, dtype=jnp.int32)
    live_count = jnp.where(jnp.arange(buffers, dtype=jnp.int32) == full_one, CAP, live_count)
    slot_ids = jnp.arange(CAP, dtype=jnp.int32)
    starts_flag = jax.random.randint(key_marks, (buffers, CAP), 0, 24, dtype=jnp.int32) == 0
    starts_flag = starts_flag | (slot_ids == 0)[None, :]
    first_slot = jnp.where(starts_flag, slot_ids[None, :], 0)
    first_slot = lax.cummax(first_slot, axis=1)
    first_slot = jnp.where(slot_ids[None, :] < live_count[:, None], first_slot, CAP)
    return first_slot.reshape(-1).astype(jnp.int32)


def block_scale(stream_key, dims, shards, least, top_value):
    def one(position, parts):
        heights = jax.random.uniform(jax.random.fold_in(jax.random.fold_in(stream_key, 6), position), (parts,), jnp.float32, least / len(shards), top_value / len(shards))
        return jnp.repeat(jnp.exp(heights), dims[position] // parts).reshape((-1,) + (1,) * (len(dims) - position - 1))

    gain = one(*shards[0])
    for cut in shards[1:]:
        gain = gain * one(*cut)
    return gain


def scatter_about(rng, shape, width, reach, cuts=(), kind=jnp.bfloat16):
    level = block_scale(rng, shape, cuts, -0.22, 0.18) if cuts else 1.0
    array = jax.random.normal(rng, shape, jnp.float32) * width * level
    return jnp.minimum(jnp.maximum(array, -reach), reach).astype(kind)


def setup_inputs(seed: int = 0) -> dict:
    keys = jax.random.split(jax.random.key(seed), 12)
    hidden_in = draw_hidden_in(jax.random.fold_in(keys[11], 71), 0)
    seg_start = draw_seg_start(jax.random.fold_in(keys[11], 71), 0)
    w_query = scatter_about(keys[2], (D * HEADS * HDIM,), D ** -0.5, 0.1875, ((0, 32),))
    w_key = scatter_about(keys[3], (D * KVH * HDIM,), D ** -0.5, 0.1875, ((0, 32),))
    w_value = scatter_about(keys[4], (D * KVH * HDIM,), D ** -0.5, 0.1875, ((0, 32),))
    w_output = scatter_about(keys[5], (HEADS * HDIM * D,), (HEADS * HDIM // 8) ** -0.5, 0.5, ((0, 32),))
    w_gate = scatter_about(keys[6], (D * FF,), D ** -0.5, 0.1875, ((0, 32),))
    w_up = scatter_about(keys[7], (D * FF,), D ** -0.5, 0.1875, ((0, 32),))
    w_down = scatter_about(keys[8], (FF * D,), (FF // 4) ** -0.5, 0.25, ((0, 32),))
    norm_gains = jnp.clip(1.0 + 0.1 * jax.random.normal(keys[9], (GAINS,), jnp.float32), 0.5, 1.5).astype(jnp.bfloat16)
    cotangent = scatter_about(keys[10], (TOKENS, D), 1.0, 6.0, ((0, 32),))
    return dict(hidden_in=hidden_in, seg_start=seg_start, w_query=w_query, w_key=w_key, w_value=w_value, w_output=w_output, w_gate=w_gate, w_up=w_up, w_down=w_down, norm_gains=norm_gains, cotangent=cotangent)


norm_eps = 1e-05

def rope_tables(starts):
    length = starts.shape[0]
    slot_ids = jnp.arange(length, dtype=jnp.int32)
    place = (slot_ids - starts).astype(jnp.float32)
    half = HDIM // 2
    inv_freq = jnp.exp(jnp.arange(half, dtype=jnp.float32) * (-math.log(100000.0) * 2.0 / HDIM))
    angles = place[:, None] * inv_freq[None, :]
    return (jnp.cos(angles)[:, None, :], jnp.sin(angles)[:, None, :])

def rotate_fwd(tensor, cos_t, sin_t):
    half = tensor.shape[-1] // 2
    first_h = tensor[..., :half]
    second_h = tensor[..., half:]
    return jnp.concatenate([first_h * cos_t - second_h * sin_t, second_h * cos_t + first_h * sin_t], axis=-1)

def rotate_back(tensor, cos_t, sin_t):
    half = tensor.shape[-1] // 2
    first_h = tensor[..., :half]
    second_h = tensor[..., half:]
    return jnp.concatenate([first_h * cos_t + second_h * sin_t, second_h * cos_t - first_h * sin_t], axis=-1)

def visible_pairs(starts):
    length = starts.shape[0]
    slot_ids = jnp.arange(length, dtype=jnp.int32)
    return (starts[:, None] == starts[None, :]) & (slot_ids[None, :] <= slot_ids[:, None])

def rms_forward(rows_in, gain_vec):
    inv_rms = lax.rsqrt(lax.optimization_barrier(jnp.mean(rows_in * rows_in, axis=1, keepdims=True)) + norm_eps)
    normed = rows_in * inv_rms
    return (normed, inv_rms, (normed * gain_vec).astype(jnp.bfloat16))

def rms_backward(grad_rows, normed, inv_rms, gain_vec):
    scaled = grad_rows * gain_vec
    gain_grad = lax.optimization_barrier(jnp.sum(grad_rows * normed, axis=0))
    back_rows = inv_rms * (scaled - normed * lax.optimization_barrier(jnp.mean(scaled * normed, axis=1, keepdims=True)))
    return (back_rows, gain_grad)

def dot_plain(left, right):
    return jnp.dot(left, right, preferred_element_type=jnp.float32)

def einsum_float(form, left, right):
    return jnp.einsum(form, left.astype(jnp.float32), right.astype(jnp.float32))

def layer(rows_in, starts, cot_rows, weight_list, gain_one, gain_two):
    query_mat, key_mat, value_mat, out_mat, gate_mat, up_mat, down_mat = weight_list
    length = rows_in.shape[0]
    groups = KVH
    ratio = HEADS // KVH
    inv_sqrt = 1.0 / math.sqrt(HDIM)
    resid = rows_in.astype(jnp.float32)
    normed_one, rms_one, input_one = rms_forward(resid, gain_one)
    cos_t, sin_t = rope_tables(starts)
    query_rot = rotate_fwd(dot_plain(input_one, query_mat).reshape(length, HEADS, HDIM), cos_t, sin_t).astype(jnp.bfloat16)
    keys_rot = rotate_fwd(dot_plain(input_one, key_mat).reshape(length, KVH, HDIM), cos_t, sin_t).astype(jnp.bfloat16)
    values_b = dot_plain(input_one, value_mat).astype(jnp.bfloat16)
    visible = visible_pairs(starts)
    query_four = query_rot.reshape(length, groups, ratio, HDIM)
    values_three = values_b.reshape(length, groups, HDIM)
    scores = einsum_float('qgrd,kgd->grqk', query_four, keys_rot) * inv_sqrt
    denom_sum = lax.optimization_barrier(jnp.sum(jnp.where(visible, jnp.exp(scores), 0.0), axis=3))
    log_total = jnp.log(denom_sum)
    probs = jnp.where(visible, jnp.exp(scores - log_total[..., None]), 0.0)
    probs_b = probs.astype(jnp.bfloat16)
    attended = einsum_float('grqk,kgd->qgrd', probs_b, values_three).reshape(length, HEADS * HDIM).astype(jnp.bfloat16)
    mixed = resid + dot_plain(attended, out_mat)
    normed_two, rms_two, input_two = rms_forward(mixed, gain_two)
    gate_pre = dot_plain(input_two, gate_mat)
    up_pre = dot_plain(input_two, up_mat)
    sigmoid_g = jax.nn.sigmoid(gate_pre)
    silu_g = gate_pre * sigmoid_g
    product = (silu_g * up_pre).astype(jnp.bfloat16)
    output = (mixed + dot_plain(product, down_mat)).astype(jnp.bfloat16)
    live_rows = (starts < length).astype(jnp.float32)[:, None]
    grad_y = cot_rows.astype(jnp.float32) * live_rows
    grad_yb = grad_y.astype(jnp.bfloat16)
    grad_down_w = dot_plain(product.T, grad_yb)
    grad_prod = dot_plain(grad_yb, down_mat.T)
    grad_gate_b = (grad_prod * up_pre * sigmoid_g * (1.0 + gate_pre * (1.0 - sigmoid_g))).astype(jnp.bfloat16)
    grad_up_b = (grad_prod * silu_g).astype(jnp.bfloat16)
    grad_gate_w = dot_plain(input_two.T, grad_gate_b)
    grad_up_w = dot_plain(input_two.T, grad_up_b)
    grad_two = dot_plain(grad_gate_b, gate_mat.T) + dot_plain(grad_up_b, up_mat.T)
    back_two, gain_two_grad = rms_backward(grad_two, normed_two, rms_two, gain_two)
    grad_mixed = grad_y + back_two
    grad_mixed_b = grad_mixed.astype(jnp.bfloat16)
    grad_out_w = dot_plain(attended.T, grad_mixed_b)
    grad_att = dot_plain(grad_mixed_b, out_mat.T).astype(jnp.bfloat16).reshape(length, groups, ratio, HDIM)
    grad_probs = einsum_float('qgrd,kgd->grqk', grad_att, values_three)
    grad_values = einsum_float('grqk,qgrd->kgd', probs_b, grad_att).reshape(length, KVH * HDIM).astype(jnp.bfloat16)
    row_delta = lax.optimization_barrier(jnp.sum(probs * grad_probs, axis=3, keepdims=True))
    grad_scores = (probs * (grad_probs - row_delta) * inv_sqrt).astype(jnp.bfloat16)
    grad_query_rot = einsum_float('grqk,kgd->qgrd', grad_scores, keys_rot).reshape(length, HEADS, HDIM)
    grad_keys_rot = einsum_float('grqk,qgrd->kgd', grad_scores, query_four)
    grad_query_b = rotate_back(grad_query_rot, cos_t, sin_t).reshape(length, HEADS * HDIM).astype(jnp.bfloat16)
    grad_keys_b = rotate_back(grad_keys_rot, cos_t, sin_t).reshape(length, KVH * HDIM).astype(jnp.bfloat16)
    grad_query_w = dot_plain(input_one.T, grad_query_b)
    grad_key_w = dot_plain(input_one.T, grad_keys_b)
    grad_value_w = dot_plain(input_one.T, grad_values)
    grad_one = dot_plain(grad_query_b, query_mat.T) + dot_plain(grad_keys_b, key_mat.T) + dot_plain(grad_values, value_mat.T)
    back_one, gain_one_grad = rms_backward(grad_one, normed_one, rms_one, gain_one)
    grad_input = grad_mixed + back_one
    grad_list = (grad_query_w, grad_key_w, grad_value_w, grad_out_w, grad_gate_w, grad_up_w, grad_down_w, gain_one_grad, gain_two_grad)
    return (output, grad_input, grad_list)

def reference(hidden_in, seg_start, w_query, w_key, w_value, w_output, w_gate, w_up, w_down, norm_gains, cotangent):
    weight_list = (w_query.reshape(D, HEADS * HDIM), w_key.reshape(D, KVH * HDIM), w_value.reshape(D, KVH * HDIM), w_output.reshape(HEADS * HDIM, D), w_gate.reshape(D, FF), w_up.reshape(D, FF), w_down.reshape(FF, D))
    gain_all = norm_gains.astype(jnp.float32)
    gain_one = gain_all[:D]
    gain_two = gain_all[D:2 * D]
    blocks_in = hidden_in.reshape(N_DP, CAP, D)
    blocks_seg = seg_start.reshape(N_DP, CAP)
    blocks_cot = cotangent.reshape(N_DP, CAP, D)
    initial = tuple((jnp.zeros(matrix.shape, jnp.float32) for matrix in weight_list))
    initial = initial + (jnp.zeros((D,), jnp.float32), jnp.zeros((D,), jnp.float32))

    def advance(running, inputs_now):
        rows_in, starts, cot_rows = inputs_now
        output, grad_input, grad_list = layer(rows_in, starts, cot_rows, weight_list, gain_one, gain_two)
        return (tuple((prior + extra for prior, extra in zip(running, grad_list))), (output, grad_input))
    totals, (outputs, grad_inputs) = lax.scan(advance, initial, (blocks_in, blocks_seg, blocks_cot))
    grad_gains = jnp.concatenate([totals[7], totals[8], jnp.zeros((GAINS - 2 * D,), jnp.float32)])
    return (outputs.reshape(TOKENS, D), grad_inputs.reshape(TOKENS, D), totals[0].reshape(-1), totals[1].reshape(-1), totals[2].reshape(-1), totals[3].reshape(-1), totals[4].reshape(-1), totals[5].reshape(-1), totals[6].reshape(-1), grad_gains)
```

```python
import math

import jax
import jax.numpy as jnp
from jax import lax
from jax.sharding import PartitionSpec as P

HDIM = 64


norm_eps = 1e-05


def rope_tables(starts):
    length = starts.shape[0]
    slot_ids = jnp.arange(length, dtype=jnp.int32)
    place = (slot_ids - starts).astype(jnp.float32)
    half = HDIM // 2
    inv_freq = jnp.exp(jnp.arange(half, dtype=jnp.float32) * (-math.log(100000.0) * 2.0 / HDIM))
    angles = place[:, None] * inv_freq[None, :]
    return (jnp.cos(angles)[:, None, :], jnp.sin(angles)[:, None, :])


def rotate_fwd(tensor, cos_t, sin_t):
    half = tensor.shape[-1] // 2
    first_h = tensor[..., :half]
    second_h = tensor[..., half:]
    return jnp.concatenate(
        [first_h * cos_t - second_h * sin_t, second_h * cos_t + first_h * sin_t], axis=-1
    )


def rotate_back(tensor, cos_t, sin_t):
    half = tensor.shape[-1] // 2
    first_h = tensor[..., :half]
    second_h = tensor[..., half:]
    return jnp.concatenate(
        [first_h * cos_t + second_h * sin_t, second_h * cos_t - first_h * sin_t], axis=-1
    )


def visible_pairs(starts):
    length = starts.shape[0]
    slot_ids = jnp.arange(length, dtype=jnp.int32)
    return (starts[:, None] == starts[None, :]) & (slot_ids[None, :] <= slot_ids[:, None])


def rms_forward(rows_in, gain_vec):
    inv_rms = lax.rsqrt(jnp.mean(rows_in * rows_in, axis=1, keepdims=True) + norm_eps)
    normed = rows_in * inv_rms
    return (normed, inv_rms, (normed * gain_vec).astype(jnp.bfloat16))


def rms_backward(grad_rows, normed, inv_rms, gain_vec):
    scaled = grad_rows * gain_vec
    gain_grad = jnp.sum(grad_rows * normed, axis=0)
    back_rows = inv_rms * (scaled - normed * jnp.mean(scaled * normed, axis=1, keepdims=True))
    return (back_rows, gain_grad)


def dot_plain(left, right):
    return jnp.dot(left, right, preferred_element_type=jnp.float32)


def dot_first(left, right):
    return lax.dot_general(
        left, right, (((0,), (0,)), ((), ())), preferred_element_type=jnp.float32
    )


def dot_last(left, right):
    return lax.dot_general(
        left, right, (((1,), (1,)), ((), ())), preferred_element_type=jnp.float32
    )


def unpack_weights(attn_full, mlp_full, width_d):
    query_mat = attn_full[0].reshape(width_d, -1)
    key_mat = attn_full[1].reshape(width_d, -1)
    value_mat = attn_full[2].reshape(width_d, -1)
    out_mat = attn_full[3].reshape(-1, width_d)
    gain_all = attn_full[4].astype(jnp.float32)
    gate_mat = mlp_full[0].reshape(width_d, -1)
    up_mat = mlp_full[1].reshape(width_d, -1)
    down_mat = mlp_full[2].reshape(-1, width_d)
    return (
        query_mat,
        key_mat,
        value_mat,
        out_mat,
        gate_mat,
        up_mat,
        down_mat,
        gain_all[:width_d],
        gain_all[width_d : 2 * width_d],
    )


def forward_pass(rows_in, starts, weight_list):
    query_mat, key_mat, value_mat, out_mat, gate_mat, up_mat, down_mat, gain_one, gain_two = (
        weight_list
    )
    length = rows_in.shape[0]
    groups = key_mat.shape[1] // HDIM
    inv_sqrt = 1.0 / math.sqrt(HDIM)
    resid = rows_in.astype(jnp.float32)
    normed_one, rms_one, input_one = rms_forward(resid, gain_one)
    cos_t, sin_t = rope_tables(starts)
    query_rot = rotate_fwd(
        dot_plain(input_one, query_mat).reshape(length, -1, HDIM), cos_t, sin_t
    ).astype(jnp.bfloat16)
    keys_rot = rotate_fwd(
        dot_plain(input_one, key_mat).reshape(length, -1, HDIM), cos_t, sin_t
    ).astype(jnp.bfloat16)
    values_b = dot_plain(input_one, value_mat).astype(jnp.bfloat16)
    visible = visible_pairs(starts)
    query_four = query_rot.reshape(length, groups, -1, HDIM)
    values_three = values_b.reshape(length, groups, HDIM)
    scores = (
        jnp.einsum("qgrd,kgd->grqk", query_four, keys_rot, preferred_element_type=jnp.float32)
        * inv_sqrt
    )
    denom_sum = jnp.sum(jnp.where(visible, jnp.exp(scores), 0.0), axis=3)
    log_total = jnp.log(denom_sum)
    probs_b = jnp.where(visible, jnp.exp(scores - log_total[..., None]), 0.0).astype(jnp.bfloat16)
    attended = jnp.einsum(
        "grqk,kgd->qgrd", probs_b, values_three, preferred_element_type=jnp.float32
    )
    attended = attended.reshape(length, -1).astype(jnp.bfloat16)
    mixed = resid + dot_plain(attended, out_mat)
    normed_two, rms_two, input_two = rms_forward(mixed, gain_two)
    gate_pre = dot_plain(input_two, gate_mat)
    up_pre = dot_plain(input_two, up_mat)
    product = (jax.nn.silu(gate_pre) * up_pre).astype(jnp.bfloat16)
    output = (mixed + dot_plain(product, down_mat)).astype(jnp.bfloat16)
    saved = (
        normed_one,
        rms_one,
        input_one,
        cos_t,
        sin_t,
        query_four,
        keys_rot,
        values_three,
        log_total,
        attended,
        normed_two,
        rms_two,
        input_two,
        gate_pre,
        up_pre,
        product,
    )
    return (saved, output)


def backward_pass(starts, cot_rows, saved, weight_list):
    query_mat, key_mat, value_mat, out_mat, gate_mat, up_mat, down_mat, gain_one, gain_two = (
        weight_list
    )
    (
        normed_one,
        rms_one,
        input_one,
        cos_t,
        sin_t,
        query_four,
        keys_rot,
        values_three,
        log_total,
        attended,
        normed_two,
        rms_two,
        input_two,
        gate_pre,
        up_pre,
        product,
    ) = saved
    length = cot_rows.shape[0]
    inv_sqrt = 1.0 / math.sqrt(HDIM)
    live_rows = (starts < length).astype(jnp.float32)[:, None]
    grad_y = cot_rows.astype(jnp.float32) * live_rows
    grad_yb = grad_y.astype(jnp.bfloat16)
    grad_prod = dot_last(grad_yb, down_mat)
    sigmoid_g = jax.nn.sigmoid(gate_pre)
    silu_g = gate_pre * sigmoid_g
    grad_gate_b = (grad_prod * up_pre * sigmoid_g * (1.0 + gate_pre * (1.0 - sigmoid_g))).astype(
        jnp.bfloat16
    )
    grad_up_b = (grad_prod * silu_g).astype(jnp.bfloat16)
    grad_two = dot_last(grad_gate_b, gate_mat) + dot_last(grad_up_b, up_mat)
    back_two, gain_two_grad = rms_backward(grad_two, normed_two, rms_two, gain_two)
    grad_mixed = grad_y + back_two
    grad_mixed_b = grad_mixed.astype(jnp.bfloat16)
    grad_att = dot_last(grad_mixed_b, out_mat).astype(jnp.bfloat16).reshape(query_four.shape)
    visible = visible_pairs(starts)
    scores = (
        jnp.einsum("qgrd,kgd->grqk", query_four, keys_rot, preferred_element_type=jnp.float32)
        * inv_sqrt
    )
    probs = jnp.where(visible, jnp.exp(scores - log_total[..., None]), 0.0)
    probs_b = probs.astype(jnp.bfloat16)
    grad_probs = jnp.einsum(
        "qgrd,kgd->grqk", grad_att, values_three, preferred_element_type=jnp.float32
    )
    grad_values = jnp.einsum(
        "grqk,qgrd->kgd", probs_b, grad_att, preferred_element_type=jnp.float32
    )
    grad_values = grad_values.reshape(length, -1).astype(jnp.bfloat16)
    row_delta = jnp.sum(probs * grad_probs, axis=3, keepdims=True)
    grad_scores = (probs * (grad_probs - row_delta) * inv_sqrt).astype(jnp.bfloat16)
    grad_query_rot = jnp.einsum(
        "grqk,kgd->qgrd", grad_scores, keys_rot, preferred_element_type=jnp.float32
    )
    grad_query_rot = grad_query_rot.reshape(length, -1, HDIM)
    grad_keys_rot = jnp.einsum(
        "grqk,qgrd->kgd", grad_scores, query_four, preferred_element_type=jnp.float32
    )
    grad_query_b = (
        rotate_back(grad_query_rot, cos_t, sin_t).reshape(length, -1).astype(jnp.bfloat16)
    )
    grad_keys_b = rotate_back(grad_keys_rot, cos_t, sin_t).reshape(length, -1).astype(jnp.bfloat16)
    grad_one = (
        dot_last(grad_query_b, query_mat)
        + dot_last(grad_keys_b, key_mat)
        + dot_last(grad_values, value_mat)
    )
    back_one, gain_one_grad = rms_backward(grad_one, normed_one, rms_one, gain_one)
    grad_input = grad_mixed + back_one
    pairs = (
        (input_one, grad_query_b),
        (input_one, grad_keys_b),
        (input_one, grad_values),
        (attended, grad_mixed_b),
        (input_two, grad_gate_b),
        (input_two, grad_up_b),
        (product, grad_yb),
    )
    return (grad_input, pairs, gain_one_grad, gain_two_grad)


def flat_block(left, right):
    block = dot_first(left, right).reshape(-1)
    return block


def shards_flat(
    hidden_in,
    seg_start,
    w_query,
    w_key,
    w_value,
    w_output,
    w_gate,
    w_up,
    w_down,
    norm_gains,
    cotangent,
):
    width_d = hidden_in.shape[1]
    attn_full = (
        lax.all_gather(w_query, "dp", axis=0, tiled=True),
        lax.all_gather(w_key, "dp", axis=0, tiled=True),
        lax.all_gather(w_value, "dp", axis=0, tiled=True),
        lax.all_gather(w_output, "dp", axis=0, tiled=True),
        lax.all_gather(norm_gains, "dp", axis=0, tiled=True),
    )
    mlp_full = (
        lax.all_gather(w_gate, "dp", axis=0, tiled=True),
        lax.all_gather(w_up, "dp", axis=0, tiled=True),
        lax.all_gather(w_down, "dp", axis=0, tiled=True),
    )
    weight_list = unpack_weights(attn_full, mlp_full, width_d)
    saved, hidden_out = forward_pass(hidden_in, seg_start, weight_list)
    grad_input, pairs, gain_one_grad, gain_two_grad = backward_pass(
        seg_start, cotangent, saved, weight_list
    )
    gain_length = attn_full[4].shape[0]
    gain_grads = jnp.concatenate(
        [gain_one_grad, gain_two_grad, jnp.zeros((gain_length - 2 * width_d,), jnp.float32)]
    )
    shard_sizes = [
        w_query.shape[0],
        w_key.shape[0],
        w_value.shape[0],
        w_output.shape[0],
        w_gate.shape[0],
        w_up.shape[0],
        w_down.shape[0],
        norm_gains.shape[0],
    ]
    stride = sum(shard_sizes)
    owners = lax.axis_size("dp") * stride // stride
    pieces = []
    for index in range(7):
        term_size_one = shard_sizes[index]
        left, right = pairs[index]
        flat_part = flat_block(left, right)
        pieces.append(flat_part.reshape(owners, term_size_one))
    pieces.append(gain_grads.reshape(owners, shard_sizes[7]))
    mine = lax.psum_scatter(
        jnp.concatenate(pieces, axis=1).reshape(-1), "dp", scatter_dimension=0, tiled=True
    )
    outputs = []
    offset = 0
    for size_one in shard_sizes:
        outputs.append(mine[offset : offset + size_one])
        offset = offset + size_one
    return (
        hidden_out,
        grad_input,
        outputs[0],
        outputs[1],
        outputs[2],
        outputs[3],
        outputs[4],
        outputs[5],
        outputs[6],
        outputs[7],
    )


SUBLANES = 16


class Ring:
    def __init__(self, size):
        self.size = size
        self.line = size // 8
        self.me = lax.axis_index("dp")

    def swap(self, array, bit):
        return lax.ppermute(array, "dp", [(i, i ^ bit) for i in range(self.size)])

    def shift(self, array, step):
        pairs = []
        for i in range(self.size):
            place, rest = divmod(i, 8)
            pairs.append((i, (place + step) % self.line * 8 + rest))
        return lax.ppermute(array, "dp", pairs)

    def owners(self, bits):
        block = jnp.arange(self.size, dtype=jnp.int32)
        along = block % self.line
        rest = block // self.line
        flip = (rest // 4) * 1 + (rest // 2 % 2) * bits[0] + (rest % 2) * bits[1]
        place = (self.me // 8 + along) % self.line
        return place * 8 + ((self.me % 8) ^ flip)

    def gather(self, rows, bits):
        near = [rows] + [self.shift(rows, -step) for step in range(1, self.line)]
        near = jnp.concatenate(near, axis=0)
        half = jnp.concatenate([near, self.swap(near, bits[1])], axis=0)
        far = self.swap(half, bits[0])
        return [half, far, self.swap(half, 1), self.swap(far, 1)]

    def scatter(self, kept, sent, bits):
        held = kept + self.swap(sent.astype(jnp.bfloat16), bits[0]).astype(jnp.float32)
        count = held.shape[0] // 2
        away = held[count:].astype(jnp.bfloat16)
        held = held[:count] + self.swap(away, bits[1]).astype(jnp.float32)
        count = held.shape[0] // self.line
        total = held[:count]
        for step in range(1, self.line):
            away = held[step * count : (step + 1) * count].astype(jnp.bfloat16)
            total = total + self.shift(away, step).astype(jnp.float32)
        return total


def pad_rows(flat, columns):
    rows = flat.reshape(-1, columns)
    extra = -rows.shape[0] % SUBLANES
    return jnp.pad(rows, ((0, extra), (0, 0)))


def placement(owners, count, total):
    padded = count + -count % SUBLANES
    row = jnp.arange(padded, dtype=jnp.int32)
    feature = jnp.where(row < count, owners[:, None] * count + row[None, :], -1).reshape(-1)
    return (jnp.arange(total, dtype=jnp.int32)[:, None] == feature[None, :]).astype(jnp.bfloat16)


def place(values, spots):
    return dot_plain(values, spots).astype(jnp.bfloat16)


def take(values, spots):
    high = values.astype(jnp.bfloat16)
    low = (values - high.astype(jnp.float32)).astype(jnp.bfloat16)
    return dot_last(high, spots) + dot_last(low, spots)


def split_columns(values, parts):
    width = values.shape[1] // len(parts)
    return [values[:, i * width : (i + 1) * width] for i in range(len(parts))]


def dot_parts(placed, parts):
    total = None
    for left, right in zip(split_columns(placed, parts), parts):
        term = dot_plain(left, right)
        total = term if total is None else total + term
    return total


def dot_back(values, parts):
    return jnp.concatenate([dot_last(values, part) for part in parts], axis=1)


def shards(
    hidden_in,
    seg_start,
    w_query,
    w_key,
    w_value,
    w_output,
    w_gate,
    w_up,
    w_down,
    norm_gains,
    cotangent,
):
    size = lax.axis_size("dp")
    width_d = hidden_in.shape[1]
    length = hidden_in.shape[0]
    row_count = w_output.shape[0] // width_d
    query_cols = w_query.shape[0] // row_count
    key_cols = w_key.shape[0] // row_count
    value_cols = w_value.shape[0] // row_count
    ff_cols = w_gate.shape[0] // row_count
    down_count = w_down.shape[0] // width_d
    groups = key_cols // HDIM
    inv_sqrt = 1.0 / math.sqrt(HDIM)
    ring = Ring(size)
    side_x, side_y = (2, 4), (4, 2)

    live_rows = (seg_start < length).astype(jnp.float32)[:, None]
    grad_y = cotangent.astype(jnp.float32) * live_rows
    grad_yb = grad_y.astype(jnp.bfloat16)

    owners_x, owners_y = ring.owners(side_x), ring.owners(side_y)
    gain_parts = ring.gather(norm_gains.reshape(1, -1), side_x)
    qkv_rows = jnp.concatenate(
        [
            pad_rows(w_query, query_cols),
            pad_rows(w_key, key_cols),
            pad_rows(w_value, value_cols),
        ],
        axis=1,
    )
    qkv_parts = ring.gather(qkv_rows, side_x)
    out_parts = ring.gather(pad_rows(w_output, width_d), side_y)
    up_parts = ring.gather(pad_rows(w_up, ff_cols), side_y)
    gate_parts = ring.gather(pad_rows(w_gate, ff_cols), side_x)
    down_parts = ring.gather(pad_rows(w_down, width_d), side_y)

    spots_x = placement(owners_x, row_count, width_d)
    spots_y = placement(owners_y, row_count, width_d)
    spots_ff = placement(owners_y, down_count, ff_cols)
    order = (jnp.arange(size, dtype=jnp.int32)[:, None] == owners_x[None, :]).astype(jnp.bfloat16)
    gain_all = dot_plain(order, jnp.concatenate(gain_parts, axis=0)).reshape(-1)
    gain_one = gain_all[:width_d]
    gain_two = gain_all[width_d : 2 * width_d]

    def with_partner(own):
        return jnp.concatenate([own, ring.swap(own, 1)], axis=0)

    def halves(placed):
        half = placed.shape[1] // 2
        return jnp.concatenate([placed[:, :half], ring.swap(placed[:, half:], 1)], axis=0)

    def reduce(left, right, bits):
        half = left.shape[1] // 2
        return ring.scatter(
            dot_first(left[:, :half], right), dot_first(left[:, half:], right), bits
        )

    resid = hidden_in.astype(jnp.float32)
    normed_one, rms_one, input_one = rms_forward(resid, gain_one)
    placed_one = place(input_one, spots_x)
    qkv = dot_parts(placed_one, qkv_parts)
    cos_t, sin_t = rope_tables(seg_start)
    query_rot = rotate_fwd(
        qkv[:, :query_cols].reshape(length, -1, HDIM), cos_t, sin_t
    ).astype(jnp.bfloat16)
    keys_rot = rotate_fwd(
        qkv[:, query_cols : query_cols + key_cols].reshape(length, -1, HDIM), cos_t, sin_t
    ).astype(jnp.bfloat16)
    values_three = (
        qkv[:, query_cols + key_cols :].astype(jnp.bfloat16).reshape(length, groups, HDIM)
    )
    visible = visible_pairs(seg_start)
    query_four = query_rot.reshape(length, groups, -1, HDIM)
    scores = (
        jnp.einsum("qgrd,kgd->grqk", query_four, keys_rot, preferred_element_type=jnp.float32)
        * inv_sqrt
    )
    denom_sum = jnp.sum(jnp.where(visible, jnp.exp(scores), 0.0), axis=3)
    log_total = jnp.log(denom_sum)
    probs = jnp.where(visible, jnp.exp(scores - log_total[..., None]), 0.0)
    probs_b = probs.astype(jnp.bfloat16)
    attended = jnp.einsum(
        "grqk,kgd->qgrd", probs_b, values_three, preferred_element_type=jnp.float32
    )
    attended = attended.reshape(length, -1).astype(jnp.bfloat16)
    placed_att = place(attended, spots_y)
    mixed = resid + dot_parts(placed_att, out_parts)
    normed_two, rms_two, input_two = rms_forward(mixed, gain_two)
    placed_gate = place(input_two, spots_x)
    placed_up = place(input_two, spots_y)
    up_pre = dot_parts(placed_up, up_parts)
    gate_pre = dot_parts(placed_gate, gate_parts)
    sigmoid_g = jax.nn.sigmoid(gate_pre)
    silu_g = gate_pre * sigmoid_g
    product = (silu_g * up_pre).astype(jnp.bfloat16)
    placed_prod = place(product, spots_ff)
    hidden_out = (mixed + dot_parts(placed_prod, down_parts)).astype(jnp.bfloat16)

    mine_down = reduce(halves(placed_prod), with_partner(grad_yb), side_y)
    grad_prod = dot_last(dot_back(grad_yb, down_parts).astype(jnp.bfloat16), spots_ff)
    grad_gate_b = (grad_prod * up_pre * sigmoid_g * (1.0 + gate_pre * (1.0 - sigmoid_g))).astype(
        jnp.bfloat16
    )
    grad_up_b = (grad_prod * silu_g).astype(jnp.bfloat16)
    mine_gate = reduce(halves(placed_gate), with_partner(grad_gate_b), side_x)
    mine_up = reduce(halves(placed_up), with_partner(grad_up_b), side_y)
    grad_two = take(dot_back(grad_gate_b, gate_parts), spots_x) + take(
        dot_back(grad_up_b, up_parts), spots_y
    )
    back_two, gain_two_grad = rms_backward(grad_two, normed_two, rms_two, gain_two)
    grad_mixed = grad_y + back_two
    grad_mixed_b = grad_mixed.astype(jnp.bfloat16)
    mine_out = reduce(halves(placed_att), with_partner(grad_mixed_b), side_y)
    grad_att = dot_last(dot_back(grad_mixed_b, out_parts).astype(jnp.bfloat16), spots_y)
    grad_att = grad_att.astype(jnp.bfloat16).reshape(query_four.shape)
    grad_probs = jnp.einsum(
        "qgrd,kgd->grqk", grad_att, values_three, preferred_element_type=jnp.float32
    )
    grad_values = jnp.einsum(
        "grqk,qgrd->kgd", probs_b, grad_att, preferred_element_type=jnp.float32
    )
    grad_values = grad_values.reshape(length, -1).astype(jnp.bfloat16)
    row_delta = jnp.sum(probs * grad_probs, axis=3, keepdims=True)
    grad_scores = (probs * (grad_probs - row_delta) * inv_sqrt).astype(jnp.bfloat16)
    grad_query_rot = jnp.einsum(
        "grqk,kgd->qgrd", grad_scores, keys_rot, preferred_element_type=jnp.float32
    ).reshape(length, -1, HDIM)
    grad_keys_rot = jnp.einsum(
        "grqk,qgrd->kgd", grad_scores, query_four, preferred_element_type=jnp.float32
    )
    grad_query_b = (
        rotate_back(grad_query_rot, cos_t, sin_t).reshape(length, -1).astype(jnp.bfloat16)
    )
    grad_keys_b = rotate_back(grad_keys_rot, cos_t, sin_t).reshape(length, -1).astype(jnp.bfloat16)
    grad_qkv = jnp.concatenate([grad_query_b, grad_keys_b, grad_values], axis=1)
    mine_qkv = reduce(halves(placed_one), with_partner(grad_qkv), side_x)
    grad_one = take(dot_back(grad_qkv, qkv_parts), spots_x)
    back_one, gain_one_grad = rms_backward(grad_one, normed_one, rms_one, gain_one)
    grad_input = grad_mixed + back_one

    gain_length = norm_gains.shape[0] * size
    gain_grads = jnp.concatenate(
        [gain_one_grad, gain_two_grad, jnp.zeros((gain_length - 2 * width_d,), jnp.float32)]
    ).reshape(size, -1)
    gain_rel = lax.dot_general(
        order.astype(jnp.float32),
        gain_grads,
        (((0,), (0,)), ((), ())),
        precision=lax.Precision.HIGHEST,
        preferred_element_type=jnp.float32,
    )
    half = size // 2
    gain_pair = gain_rel[:half] + ring.swap(gain_rel[half:], 1)
    mine_gain = ring.scatter(gain_pair[: half // 2], gain_pair[half // 2 :], side_x)

    mine_qkv = mine_qkv[:row_count]
    return (
        hidden_out,
        grad_input,
        mine_qkv[:, :query_cols].reshape(-1),
        mine_qkv[:, query_cols : query_cols + key_cols].reshape(-1),
        mine_qkv[:, query_cols + key_cols :].reshape(-1),
        mine_out[:row_count].reshape(-1),
        mine_gate[:row_count].reshape(-1),
        mine_up[:row_count].reshape(-1),
        mine_down[:down_count].reshape(-1),
        mine_gain.reshape(-1),
    )


def dispatch(*arrays):
    size = lax.axis_size("dp")
    width_d = arrays[0].shape[1]
    ff_total = arrays[8].shape[0] * size // width_d
    if size % 8 == 0 and width_d % size == 0 and ff_total % (size * SUBLANES) == 0:
        return shards(*arrays)
    return shards_flat(*arrays)


def solution(mesh):
    return jax.shard_map(
        dispatch,
        mesh=mesh,
        in_specs=(
            P("dp", None),
            P("dp"),
            P("dp"),
            P("dp"),
            P("dp"),
            P("dp"),
            P("dp"),
            P("dp"),
            P("dp"),
            P("dp"),
            P("dp", None),
        ),
        out_specs=(
            P("dp", None),
            P("dp", None),
            P("dp"),
            P("dp"),
            P("dp"),
            P("dp"),
            P("dp"),
            P("dp"),
            P("dp"),
            P("dp"),
        ),
        check_vma=False,
    )
```
